32 devices in a mesh: seq: 4 (over y, x), tp: 8 (over z, core).
Axes of the slice: x: 2, y: 2, z: 4, core: 2. Of those that a mesh axis runs over, the one named last changes fastest.
Arguments:
- hidden: bfloat16 [4096, 4096], P(('seq', 'tp')), may hold values from -6 to 6
- norm_gain: float32 [4096], replicated, may hold values from 0.5 to 1.5
- inner_weight: bfloat16 [4096, 2, 2048], P(None, None, 'tp'), may hold values from -0.09375 to 0.09375
- group_weight: bfloat16 [4096, 1024], P(None, 'tp'), may hold values from -0.09375 to 0.09375
- step_weight: bfloat16 [4096, 32], P(None, 'tp'), may hold values from -0.09375 to 0.09375
- step_bias: float32 [32], P('tp'), may hold values from -2 to 1
- decay_rate: float32 [32], P('tp'), may hold values from 0.0001 to 0.1
- filter_inner: bfloat16 [4, 2048], P(None, 'tp'), may hold values from -3 to 3
- filter_group: bfloat16 [4, 1024], P(None, 'tp'), may hold values from -3 to 3
- skip_gain: float32 [32], P('tp'), may hold values from 0.5 to 1.5
- mixer_gain: float32 [2048], P('tp'), may hold values from 0.5 to 1.5
- output_weight: bfloat16 [2048, 4096], P('tp'), may hold values from -0.125 to 0.125
- segment_ids: int32 [4096], replicated, may hold values from 0 to 3, never falling along the last dimension, each value on 1 to 2048 neighbouring positions
Outputs:
- layer_out: bfloat16 [4096, 4096], P(('seq', 'tp'))
The draws below stay inside these ranges and needn't reach their ends.
Inputs may be any that keep to these rules, and one draw needn't show every extreme that they name: `segment_ids`: ids never fall along the pack; every id names at least one token, and one request has exactly 2048 tokens.
All inputs are finite; a program needn't handle non-finite values.
Results may differ from the reference program's by a relative error of at most 0.0051.
Values may be sent and summed in bfloat16 or wider, within the bound.
A program may use at most 128 MiB of HBM per device.

```python
import math
import jax
import jax.numpy as jnp
import numpy as np
from jax import lax

D = 4096
HEAD_DIM = 64
STATE = 128
CONV = 4
REQS = 4
HEADS = 32
GROUPS = 4
INNER = 2048
TOKENS = 4096
LONGEST = 2048


def level_of(rng, shape, cuts, smallest, largest):
    level = 1.0
    for dim, shards_of in cuts:
        draws = jax.random.uniform(jax.random.fold_in(jax.random.fold_in(rng, 6), dim), (shards_of,), jnp.float32, smallest / len(cuts), largest / len(cuts))
        level = level * jnp.repeat(jnp.exp(draws), shape[dim] // shards_of).reshape((-1,) + (1,) * (len(shape) - 1 - dim))
    return level


def length_profile(amount, total, limit, slope):
    loads = [(1 << 20) // math.isqrt(standing ** slope) + 1 for standing in range(2, amount + 1)]
    surplus, given = total - limit - (amount - 1), [1] * (amount - 1)
    while surplus > 0:
        movable = [i for i in range(amount - 1) if given[i] < limit]
        mass, remaining = sum([loads[i] for i in movable]), surplus
        for i in movable:
            more = min(limit - given[i], max(1, remaining * loads[i] // mass), surplus)
            given[i] = given[i] + more
            surplus = surplus - more
    return np.array([limit] + given)


def ragged_sizes(key, amount, total, bound, slope):
    if amount == 2:
        one = jax.random.randint(key, (), max(1, total - bound), min(bound, total - 1) + 1)
        return jnp.stack([one, total - one])
    lengths = jnp.asarray(length_profile(amount, total, bound, slope), jnp.int32)
    couples = (amount - 1) // 2
    donor, sink = lengths[1:1 + 2 * couples:2], lengths[2:2 + 2 * couples:2]
    room = jnp.minimum(donor - 1, bound - sink)
    shifted = jax.random.randint(jax.random.fold_in(key, 1), (couples,), 0, 1 << 20) % (room + 1)
    lengths = lengths.at[1:1 + 2 * couples:2].set(donor - shifted).at[2:2 + 2 * couples:2].set(sink + shifted)
    return lengths[jax.random.permutation(jax.random.fold_in(key, 2), amount)]


def bell_draw(key, extent, scale, most, shards=(), dtype=jnp.bfloat16):
    result = scale * jax.random.normal(key, extent, jnp.float32)
    if shards:
        result = result * level_of(key, extent, shards, -0.22, 0.18)
    return jnp.clip(result, -most, most).astype(dtype)


def setup_inputs(seed: int = 0) -> dict:
    arg_keys = jax.random.split(jax.random.key(seed), 14)
    hidden = bell_draw(arg_keys[0], (TOKENS, D), 1.0, 6.0, ((0, 32),))
    norm_gain = jnp.clip(1.0 + 0.1 * jax.random.normal(arg_keys[1], (D,), jnp.float32), 0.5, 1.5)
    inner_weight = bell_draw(arg_keys[2], (D, 2, INNER), D ** -0.5, 0.09375, ((2, 8),))
    group_weight = bell_draw(arg_keys[3], (D, GROUPS * 2 * STATE), D ** -0.5, 0.09375, ((1, 8),))
    step_weight = bell_draw(arg_keys[4], (D, HEADS), D ** -0.5, 0.09375, ((1, 8),))
    step_bias = jnp.clip(-2.0 + 3.0 * jax.random.uniform(arg_keys[5], (HEADS,), jnp.float32) ** level_of(arg_keys[5], (HEADS,), ((0, 8),), -0.2, 0.2), -2.0, 1.0)
    decay_rate = jnp.clip(jnp.exp(math.log(0.1) - 6.9077553 * jax.random.uniform(arg_keys[6], (HEADS,), jnp.float32) ** level_of(arg_keys[6], (HEADS,), ((0, 8),), -0.2, 0.2)), 0.0001, 0.1)
    filter_inner = bell_draw(arg_keys[7], (CONV, INNER), CONV ** -0.5, 3.0, ((1, 8),))
    filter_group = bell_draw(arg_keys[8], (CONV, GROUPS * 2 * STATE), CONV ** -0.5, 3.0, ((1, 8),))
    skip_gain = jnp.clip(0.5 + 1.0 * jax.random.uniform(arg_keys[9], (HEADS,), jnp.float32) ** level_of(arg_keys[9], (HEADS,), ((0, 8),), -0.2, 0.2), 0.5, 1.5)
    mixer_gain = jnp.clip(1.0 + 0.1 * jax.random.normal(arg_keys[10], (INNER,), jnp.float32), 0.5, 1.5)
    output_weight = bell_draw(arg_keys[11], (INNER, D), INNER ** -0.5, 0.125, ((0, 8),))
    segment_ids = jnp.searchsorted(jnp.cumsum(ragged_sizes(arg_keys[12], REQS, TOKENS, LONGEST, 2)), jnp.arange(TOKENS), side="right").astype(jnp.int32)
    return dict(hidden=hidden, norm_gain=norm_gain, inner_weight=inner_weight, group_weight=group_weight, step_weight=step_weight, step_bias=step_bias, decay_rate=decay_rate, filter_inner=filter_inner, filter_group=filter_group, skip_gain=skip_gain, mixer_gain=mixer_gain, output_weight=output_weight, segment_ids=segment_ids)


EPS = 1e-05

def reference(hidden, norm_gain, inner_weight, group_weight, step_weight, step_bias, decay_rate, filter_inner, filter_group, skip_gain, mixer_gain, output_weight, segment_ids):
    hidden_f = hidden.astype(jnp.float32)
    normed = (hidden_f * lax.rsqrt(lax.optimization_barrier(jnp.mean(hidden_f * hidden_f, axis=-1, keepdims=True)) + EPS) * norm_gain).astype(jnp.bfloat16)
    gate_in = jnp.dot(normed, inner_weight.reshape(D, 2 * INNER), preferred_element_type=jnp.float32)
    gate_z = gate_in[:, :INNER]
    maps_in = jnp.dot(normed, group_weight, preferred_element_type=jnp.float32)
    step_raw = jnp.dot(normed, step_weight, preferred_element_type=jnp.float32)
    conv_in = jnp.concatenate([gate_in[:, INNER:], maps_in], axis=1)
    filters = jnp.concatenate([filter_inner, filter_group], axis=1).astype(jnp.float32)
    padded = jnp.pad(conv_in, ((CONV - 1, 0), (0, 0)))
    seg_pad = jnp.concatenate([jnp.full((CONV - 1,), -1, jnp.int32), segment_ids.astype(jnp.int32)])
    total = jnp.zeros_like(conv_in)
    for offset in range(CONV):
        same = (seg_pad[offset:offset + TOKENS] == segment_ids).astype(jnp.float32)
        total = total + filters[offset] * padded[offset:offset + TOKENS] * same[:, None]
    active = jax.nn.silu(total)
    inner_x = active[:, :INNER].reshape(TOKENS, HEADS, HEAD_DIM)
    grouped_maps = active[:, INNER:].reshape(TOKENS, GROUPS, 2, STATE)
    input_map = grouped_maps[:, :, 0]
    output_map = grouped_maps[:, :, 1]
    step = jax.nn.softplus(step_raw + step_bias)
    log_decay = -step * decay_rate
    starts = jnp.concatenate([jnp.ones((1,), jnp.bool_), segment_ids[1:] != segment_ids[:-1]])
    per_group = HEADS // GROUPS

    def advance(state, inputs):
        token_x, token_b, token_c, token_step, token_log, token_start = inputs
        keep = jnp.where(token_start, 0.0, jnp.exp(token_log))
        wide_b = jnp.repeat(token_b, per_group, axis=0)
        wide_c = jnp.repeat(token_c, per_group, axis=0)
        state = keep[:, None, None] * state + (token_step[:, None] * token_x)[:, :, None] * wide_b[:, None, :]
        read = jnp.einsum('hpn,hn->hp', state, wide_c, precision=lax.Precision.HIGHEST)
        return (state, read)
    initial = jnp.zeros((HEADS, HEAD_DIM, STATE), jnp.float32)
    _, scanned = lax.scan(advance, initial, (inner_x, input_map, output_map, step, log_decay, starts))
    ssm_out = scanned + skip_gain[None, :, None] * inner_x
    gated = ssm_out.reshape(TOKENS, INNER) * jax.nn.silu(gate_z)
    by_group = gated.reshape(TOKENS, GROUPS, INNER // GROUPS)
    scaled = by_group * lax.rsqrt(lax.optimization_barrier(jnp.mean(by_group * by_group, axis=-1, keepdims=True)) + EPS)
    mixed = (scaled.reshape(TOKENS, INNER) * mixer_gain).astype(jnp.bfloat16)
    return (hidden_f + jnp.dot(mixed, output_weight, preferred_element_type=jnp.float32)).astype(jnp.bfloat16)
```

```python
import jax
import jax.numpy as jnp
from jax import lax
from jax.sharding import PartitionSpec as P

STRETCH = 256


EPS = 1e-05
HIGH = lax.Precision.HIGHEST


def swapped(block, axis, stride):
    count = lax.axis_size(axis)
    route = []
    for low in range(count):
        high = low | 1 << stride
        if high != low and high < count:
            route += [(low, high), (high, low)]
    return lax.ppermute(block, axis, route)


def crossed(block, axis, mask):
    if mask == 0:
        return block
    return lax.ppermute(block, axis, [(i, i ^ mask) for i in range(lax.axis_size(axis))])


def tail_of_previous(block):
    spans, parts = lax.axis_size("seq"), lax.axis_size("tp")
    total = None
    for part in range(parts):
        route = [(i * parts - 1, i * parts + part) for i in range(1, spans)]
        got = lax.ppermute(block, ("seq", "tp"), route)
        total = got if total is None else total + got
    return total


def spread_weight(weight, spans, chips):
    cols = weight.shape[1] // spans
    own = lax.dynamic_slice_in_dim(weight, lax.axis_index("seq") * cols, cols, axis=1)
    along = [crossed(own, "tp", 2 * d) for d in range(chips)]
    return [[crossed(part, "seq", e) for part in along] for e in range(spans)]


def entering_2(value, axis, join, neutral):
    count, mine = (lax.axis_size(axis), lax.axis_index(axis))
    pieces = jax.tree.map(lambda part: lax.all_gather(part, axis), value)
    total = jax.tree.map(
        lambda part, zero: jnp.full_like(part, 0) + jnp.asarray(zero, part.dtype), value, neutral
    )

    def hop(position, total):
        longer = join(total, jax.tree.map(lambda part: part[position], pieces))
        return jax.tree.map(lambda new, old: jnp.where(position < mine, new, old), longer, total)

    return lax.fori_loop(0, count - 1, hop, total)


def combine(earlier, later):
    return (earlier[0] * later[0], later[0][:, None, None] * earlier[1] + later[1])


def project_out(hidden, mixed, weights):
    rows, spans, chips = hidden.shape[0], len(weights), len(weights[0])
    chip, core = lax.axis_index("tp") // 2, lax.axis_index("tp") % 2
    span = lax.axis_index("seq")
    cols = hidden.shape[1] // spans
    taken = []
    for d in range(chips):
        block = lax.dynamic_slice_in_dim(mixed, (chip ^ d) * 2 * rows, 2 * rows, axis=0)
        taken.append(crossed(block, "tp", 2 * d))
    out = jnp.zeros(hidden.shape, jnp.bfloat16)
    for e in range(spans):
        part = sum(
            jnp.dot(m, w, preferred_element_type=jnp.float32) for m, w in zip(taken, weights[e])
        )
        own = lax.dynamic_slice_in_dim(part, core * rows, rows, axis=0)
        other = lax.dynamic_slice_in_dim(part, (1 - core) * rows, rows, axis=0)
        other = crossed(other.astype(jnp.bfloat16), "tp", 1).astype(jnp.float32)
        start = (span ^ e) * cols
        base = lax.dynamic_slice_in_dim(hidden, start, cols, axis=1).astype(jnp.float32)
        done = (base + own + other).astype(jnp.bfloat16)
        out = lax.dynamic_update_slice_in_dim(out, done, start, axis=1)
    return out


def body(
    hidden,
    norm_gain,
    inner_weight,
    group_weight,
    step_weight,
    step_bias,
    decay_rate,
    filter_inner,
    filter_group,
    skip_gain,
    mixer_gain,
    output_weight,
    segment_ids,
):
    rows = hidden.shape[0]
    length = rows * lax.axis_size("tp")
    width = hidden.shape[1]
    inner_dev = inner_weight.shape[2]
    heads_dev = step_weight.shape[1]
    head_dim = inner_dev // heads_dev
    state_dim = group_weight.shape[1]
    taps = filter_inner.shape[0]
    first_row = lax.axis_index("seq") * length
    is_first = lax.axis_index("tp") % 2 == 0
    hidden_f = hidden.astype(jnp.float32)
    normed = (
        hidden_f
        * lax.rsqrt(jnp.mean(hidden_f * hidden_f, axis=-1, keepdims=True) + EPS)
        * norm_gain
    ).astype(jnp.bfloat16)
    other_weight, other_filter = swapped((group_weight, filter_group), "tp", 0)
    group_cols = (
        jnp.where(is_first, group_weight, other_weight),
        jnp.where(is_first, other_weight, group_weight),
    )
    filters = jnp.concatenate(
        [
            filter_inner,
            jnp.where(is_first, filter_group, other_filter),
            jnp.where(is_first, other_filter, filter_group),
        ],
        axis=1,
    )
    spans, chips = lax.axis_size("seq"), lax.axis_size("tp") // 2
    weights = spread_weight(output_weight, spans, chips)
    tail = tail_of_previous(normed[rows - 8 :])
    matrix = jnp.concatenate(
        (inner_weight.reshape(width, 2 * inner_dev),)
        + group_cols
        + (jnp.pad(step_weight, ((0, 0), (0, 128 - heads_dev))),),
        axis=1,
    )
    before = jnp.dot(tail, matrix[:, inner_dev:-128], preferred_element_type=jnp.float32)
    before = before[8 - (taps - 1) :]
    piece = lax.all_gather(normed, "tp", axis=0, tiled=True)
    projected = jnp.dot(piece, matrix, preferred_element_type=jnp.float32)
    gate_z = projected[:, :inner_dev]
    conv_in = projected[:, inner_dev:-128]
    step_raw = projected[:, -128 : heads_dev - 128]
    seg_pad = jnp.concatenate([jnp.full((taps - 1,), -1, jnp.int32), segment_ids])
    seg_ext = lax.dynamic_slice_in_dim(seg_pad, first_row, length + taps - 1)
    seg_local = seg_ext[taps - 1 :]
    extended = jnp.concatenate([before, conv_in], axis=0)
    filters_f = filters.astype(jnp.float32)
    total = jnp.zeros_like(conv_in)
    for offset in range(taps):
        same = (seg_ext[offset : offset + length] == seg_local).astype(jnp.float32)
        total = total + filters_f[offset] * extended[offset : offset + length] * same[:, None]
    active = jax.nn.silu(total)
    inner_x = active[:, :inner_dev]
    input_map = active[:, inner_dev : inner_dev + state_dim]
    output_map = active[:, inner_dev + state_dim :]
    starts = seg_local != seg_ext[taps - 2 : taps - 2 + length]
    step = jax.nn.softplus(step_raw + step_bias)
    log_decay = -step * decay_rate
    blocks = length // STRETCH
    block_x = inner_x.reshape(blocks, STRETCH, heads_dev, head_dim)
    block_b = input_map.reshape(blocks, STRETCH, state_dim)
    block_c = output_map.reshape(blocks, STRETCH, state_dim)
    step_heads = step.reshape(blocks, STRETCH, heads_dev).transpose(0, 2, 1)
    cumul = jnp.cumsum(log_decay.reshape(blocks, STRETCH, heads_dev), axis=1).transpose(0, 2, 1)
    block_seg = seg_local.reshape(blocks, STRETCH)
    block_start = starts.reshape(blocks, STRETCH)
    causal = jnp.tril(jnp.ones((STRETCH, STRETCH), jnp.bool_))
    same_seg = ((block_seg[:, :, None] == block_seg[:, None, :]) & causal)[:, None]
    gaps = cumul[:, :, :, None] - cumul[:, :, None, :]
    decay = jnp.where(same_seg, jnp.exp(jnp.where(same_seg, gaps, 0.0)), 0.0)
    products = jnp.einsum("cin,cjn->cij", block_c, block_b, precision=HIGH)
    mixing = decay * products[:, None] * step_heads[:, :, None, :]
    local_y = jnp.einsum("chij,cjhp->cihp", mixing, block_x, precision=HIGH)
    same_last = (block_seg == block_seg[:, -1:])[:, None, :]
    last_gap = cumul[:, :, -1:] - cumul
    end_weight = (
        jnp.where(same_last, jnp.exp(jnp.where(same_last, last_gap, 0.0)), 0.0) * step_heads
    )
    block_state = jnp.einsum("chj,cjhp,cjn->chpn", end_weight, block_x, block_b, precision=HIGH)
    clean = jnp.logical_not(jnp.any(block_start, axis=1)).astype(jnp.float32)
    block_keep = jnp.exp(cumul[:, :, -1]) * clean[:, None]

    def carry_blocks(carry, inputs):
        acc_state, acc_keep = carry
        keep, fresh = inputs
        return ((keep[:, None, None] * acc_state + fresh, acc_keep * keep), (acc_state, acc_keep))

    empty_state = jnp.zeros((heads_dev, head_dim, state_dim), jnp.float32)
    unit_keep = jnp.ones((heads_dev,), jnp.float32)
    (device_state, device_keep), (prior_state, prior_keep) = lax.scan(
        carry_blocks, (empty_state, unit_keep), (block_keep, block_state)
    )
    entering = entering_2((device_keep, device_state), "seq", combine, (unit_keep, empty_state))
    incoming = entering[1]
    entry_state = prior_state + prior_keep[:, :, None, None] * incoming[None]
    alive = (jnp.cumsum(block_start.astype(jnp.int32), axis=1) == 0).astype(jnp.float32)
    entry_weight = jnp.exp(cumul) * alive[:, None, :]
    carried_y = jnp.einsum("chi,cin,chpn->cihp", entry_weight, block_c, entry_state, precision=HIGH)
    ssm_out = (local_y + carried_y).reshape(length, heads_dev, head_dim) + skip_gain[
        None, :, None
    ] * inner_x.reshape(length, heads_dev, head_dim)
    gated = ssm_out.reshape(length, inner_dev) * jax.nn.silu(gate_z)
    own_squares = jnp.sum(gated * gated, axis=-1)
    other_squares = swapped(own_squares, "tp", 0)
    group_mean = (own_squares + other_squares) / (2 * inner_dev)
    mixed = (gated * lax.rsqrt(group_mean + EPS)[:, None] * mixer_gain).astype(jnp.bfloat16)
    return project_out(hidden, mixed, weights)


def solution(mesh):
    in_specs = (
        P(("seq", "tp"), None),
        P(),
        P(None, None, "tp"),
        P(None, "tp"),
        P(None, "tp"),
        P("tp"),
        P("tp"),
        P(None, "tp"),
        P(None, "tp"),
        P("tp"),
        P("tp"),
        P("tp", None),
        P(),
    )
    out_specs = P(("seq", "tp"), None)
    return jax.shard_map(body, mesh=mesh, in_specs=in_specs, out_specs=out_specs, check_vma=False)
```

```python
import jax
import jax.numpy as jnp
from jax import lax
from jax.experimental import pallas as pl
from jax.experimental.pallas import tpu as pltpu
from jax.sharding import PartitionSpec as P

STRETCH = 128
LANES = 128


EPS = 1e-05
HIGH = lax.Precision.HIGHEST


def swapped(block, axis, stride):
    count = lax.axis_size(axis)
    route = []
    for low in range(count):
        high = low | 1 << stride
        if high != low and high < count:
            route += [(low, high), (high, low)]
    return lax.ppermute(block, axis, route)


def crossed(block, axis, mask):
    if mask == 0:
        return block
    return lax.ppermute(block, axis, [(i, i ^ mask) for i in range(lax.axis_size(axis))])


def tail_of_previous(block):
    spans, parts = lax.axis_size("seq"), lax.axis_size("tp")
    total = None
    for part in range(parts):
        route = [(i * parts - 1, i * parts + part) for i in range(1, spans)]
        got = lax.ppermute(block, ("seq", "tp"), route)
        total = got if total is None else total + got
    return total


def spread_weight(weight, spans, chips):
    cols = weight.shape[1] // spans
    own = lax.dynamic_slice_in_dim(weight, lax.axis_index("seq") * cols, cols, axis=1)
    along = [crossed(own, "tp", 2 * d) for d in range(chips)]
    return [[crossed(part, "seq", e) for part in along] for e in range(spans)]


def silu(v):
    return v / (1.0 + jnp.exp(-v))


def widen(cols, heads, head_dim):
    rows = cols.shape[0]
    parts = [jnp.broadcast_to(cols[:, h : h + 1], (rows, head_dim)) for h in range(heads)]
    return jnp.concatenate(parts, axis=1)


def dot16(a, b, dims=((1,), (0,))):
    a, b = a.astype(jnp.bfloat16), b.astype(jnp.bfloat16)
    return lax.dot_general(a, b, (dims, ((), ())), preferred_element_type=jnp.float32)


def scan_kernel(
    heads, proj, before, aux, row_seg, taps, bias, rate, skip, y_out, c_out, w_out, s_out,
    edge, state, total,
):
    size, inner = y_out.shape
    states = c_out.shape[1]
    head_dim = inner // heads
    step_at = pl.program_id(0)

    @pl.when(step_at == 0)
    def _():
        edge[...] = before[...]
        state[...] = jnp.zeros_like(state)
        total[...] = jnp.zeros_like(total)

    conv = inner + 2 * states
    cur = proj[:, :conv]
    both = jnp.concatenate([edge[...], cur], axis=0)
    edge[...] = cur[size - 8 :]
    tap = taps[...]
    count = tap.shape[0]
    acc = tap[count - 1 : count] * cur
    for back in range(1, count):
        same = aux[:, back : back + 1]
        acc += tap[count - 1 - back : count - back] * both[8 - back : 8 - back + size] * same
    active = silu(acc)
    x = active[:, :inner]
    b_map = active[:, inner : inner + states]
    c_map = active[:, inner + states :]
    raw = proj[:, conv + inner :] + bias[...]
    step = jnp.maximum(raw, 0.0) + jnp.log1p(jnp.exp(-jnp.abs(raw)))
    log_decay = -step * rate[...]
    row_at = lax.broadcasted_iota(jnp.int32, (size, size), 0)
    col_at = lax.broadcasted_iota(jnp.int32, (size, size), 1)
    causal = row_at >= col_at
    cum = jnp.dot(
        causal.astype(jnp.float32), log_decay, precision=HIGH, preferred_element_type=jnp.float32
    )
    cum_rows = cum.T
    alive, in_last, alive_span = aux[:, 4:5], aux[:, 5:6], aux[:, 6:7]
    last = cum[size - 1 :]
    mask = causal & (aux[:, 0:1] == row_seg[0:1, :])
    xs = x * widen(step, heads, head_dim)
    xs16 = xs.astype(jnp.bfloat16)
    products = dot16(c_map, b_map, ((1,), (1,)))
    parts = []
    for h in range(heads):
        gap = cum[:, h : h + 1] - cum_rows[h : h + 1, :]
        mixing = products * jnp.exp(jnp.where(mask, gap, -1e30))
        parts.append(dot16(mixing, xs16[:, h * head_dim : (h + 1) * head_dim]))
    local = jnp.concatenate(parts, axis=1)
    entry = jnp.exp(cum) * alive
    carried = dot16(c_map, state[...]) * widen(entry, heads, head_dim)
    y_out[...] = local + carried + skip[...] * x
    c_out[...] = c_map.astype(jnp.bfloat16)
    w_span = jnp.exp(cum + total[...]) * alive_span
    w_out[...] = w_span
    end = jnp.exp(last - cum) * in_last
    fresh = dot16(b_map, xs * widen(end, heads, head_dim), ((0,), (0,)))
    state[...] = widen(entry[size - 1 :], heads, head_dim) * state[...] + fresh
    total[...] = total[...] + last

    @pl.when(step_at == pl.num_programs(0) - 1)
    def _():
        s_out[0:states] = state[...]
        s_out[states:] = jnp.broadcast_to(
            widen(w_span[size - 1 :], heads, head_dim), (8, inner)
        )


def local_scan(heads, states, proj, before, aux, row_seg, taps, bias, rate, skip):
    length = proj.shape[0]
    inner = skip.shape[1]
    whole = lambda a: pl.BlockSpec(a.shape, lambda i: (0,) * a.ndim)
    rows = lambda n: pl.BlockSpec((STRETCH, n), lambda i: (i, 0))
    return pl.pallas_call(
        lambda *refs: scan_kernel(heads, *refs),
        grid=(length // STRETCH,),
        in_specs=[
            rows(proj.shape[1]),
            whole(before),
            rows(aux.shape[1]),
            pl.BlockSpec((8, STRETCH), lambda i: (0, i)),
            whole(taps),
            whole(bias),
            whole(rate),
            whole(skip),
        ],
        out_specs=[
            rows(inner),
            rows(states),
            rows(LANES),
            pl.BlockSpec((states + 8, inner), lambda i: (0, 0)),
        ],
        out_shape=[
            jax.ShapeDtypeStruct((length, inner), jnp.float32),
            jax.ShapeDtypeStruct((length, states), jnp.bfloat16),
            jax.ShapeDtypeStruct((length, LANES), jnp.float32),
            jax.ShapeDtypeStruct((states + 8, inner), jnp.float32),
        ],
        scratch_shapes=[
            pltpu.VMEM((8, inner + 2 * states), jnp.float32),
            pltpu.VMEM((states, inner), jnp.float32),
            pltpu.VMEM((1, LANES), jnp.float32),
        ],
        compiler_params=pltpu.CompilerParams(vmem_limit_bytes=32 << 20),
        cost_estimate=pl.CostEstimate(
            flops=12_000_000_000, bytes_accessed=8_000_000, transcendentals=4_000_000
        ),
        name="local_scan",
    )(proj, before, aux, row_seg, taps, bias, rate, skip)


def gate_kernel(heads, y, c, w, gate, state, gated_out, sq_out):
    head_dim = y.shape[1] // heads
    carried = dot16(c[...], state[...]) * widen(w[...], heads, head_dim)
    gated = (y[...] + carried) * silu(gate[...])
    gated_out[...] = gated
    sq_out[...] = jnp.sum(gated * gated, axis=1, keepdims=True)


def gate_all(heads, y, c, w, proj, gate_block, state):
    length, inner = y.shape
    size = 256
    rows = lambda n: pl.BlockSpec((size, n), lambda i: (i, 0))
    return pl.pallas_call(
        lambda *refs: gate_kernel(heads, *refs),
        grid=(length // size,),
        in_specs=[
            rows(inner),
            rows(c.shape[1]),
            rows(LANES),
            pl.BlockSpec((size, inner), lambda i: (i, gate_block)),
            pl.BlockSpec(state.shape, lambda i: (0, 0)),
        ],
        out_specs=[rows(inner), rows(1)],
        out_shape=[
            jax.ShapeDtypeStruct((length, inner), jnp.float32),
            jax.ShapeDtypeStruct((length, 1), jnp.float32),
        ],
        compiler_params=pltpu.CompilerParams(vmem_limit_bytes=32 << 20),
        name="gate_all",
    )(y, c, w, proj, state)


def entering_state(packed, states):
    spans = lax.axis_size("seq")
    got = [
        lax.ppermute(packed, "seq", [(i, i + e) for i in range(spans - e)])
        for e in range(1, spans)
    ]
    total = jnp.zeros((states, packed.shape[1]), jnp.float32)
    for part in reversed(got):
        total = part[:states] + part[states : states + 1] * total
    return total


def project_out(hidden, mixed, weights):
    rows, spans, chips = hidden.shape[0], len(weights), len(weights[0])
    chip, core = lax.axis_index("tp") // 2, lax.axis_index("tp") % 2
    span = lax.axis_index("seq")
    cols = hidden.shape[1] // spans
    taken = []
    for d in range(chips):
        block = lax.dynamic_slice_in_dim(mixed, (chip ^ d) * 2 * rows, 2 * rows, axis=0)
        taken.append(crossed(block, "tp", 2 * d))
    out = jnp.zeros(hidden.shape, jnp.bfloat16)
    for e in range(spans):
        part = sum(
            jnp.dot(m, w, preferred_element_type=jnp.float32) for m, w in zip(taken, weights[e])
        )
        own = lax.dynamic_slice_in_dim(part, core * rows, rows, axis=0)
        other = lax.dynamic_slice_in_dim(part, (1 - core) * rows, rows, axis=0)
        other = crossed(other.astype(jnp.bfloat16), "tp", 1).astype(jnp.float32)
        start = (span ^ e) * cols
        base = lax.dynamic_slice_in_dim(hidden, start, cols, axis=1).astype(jnp.float32)
        done = (base + own + other).astype(jnp.bfloat16)
        out = lax.dynamic_update_slice_in_dim(out, done, start, axis=1)
    return out


def body(
    hidden,
    norm_gain,
    inner_weight,
    group_weight,
    step_weight,
    step_bias,
    decay_rate,
    filter_inner,
    filter_group,
    skip_gain,
    mixer_gain,
    output_weight,
    segment_ids,
):
    rows = hidden.shape[0]
    length = rows * lax.axis_size("tp")
    width = hidden.shape[1]
    inner_dev = inner_weight.shape[2]
    heads_dev = step_weight.shape[1]
    head_dim = inner_dev // heads_dev
    state_dim = group_weight.shape[1]
    taps = filter_inner.shape[0]
    first_row = lax.axis_index("seq") * length
    is_first = lax.axis_index("tp") % 2 == 0
    hidden_f = hidden.astype(jnp.float32)
    normed = (
        hidden_f
        * lax.rsqrt(jnp.mean(hidden_f * hidden_f, axis=-1, keepdims=True) + EPS)
        * norm_gain
    ).astype(jnp.bfloat16)
    other_weight, other_filter = swapped((group_weight, filter_group), "tp", 0)
    group_cols = (
        jnp.where(is_first, group_weight, other_weight),
        jnp.where(is_first, other_weight, group_weight),
    )
    filters = jnp.concatenate(
        [
            filter_inner,
            jnp.where(is_first, filter_group, other_filter),
            jnp.where(is_first, other_filter, filter_group),
        ],
        axis=1,
    )
    spans, chips = lax.axis_size("seq"), lax.axis_size("tp") // 2
    weights = spread_weight(output_weight, spans, chips)
    tail = tail_of_previous(normed[rows - 8 :])
    pad_heads = ((0, 0), (0, LANES - heads_dev))
    matrix = jnp.concatenate(
        (inner_weight[:, 1, :],)
        + group_cols
        + (inner_weight[:, 0, :], jnp.pad(step_weight, pad_heads)),
        axis=1,
    )
    conv_dim = inner_dev + 2 * state_dim
    before = jnp.dot(tail, matrix[:, :conv_dim], preferred_element_type=jnp.float32)
    seg_pad = jnp.concatenate([jnp.full((taps - 1,), -1, jnp.int32), segment_ids])
    seg_ext = lax.dynamic_slice_in_dim(seg_pad, first_row, length + taps - 1)
    seg = seg_ext[taps - 1 :]
    span_before = seg_ext[taps - 2]
    chunked = seg.reshape(-1, STRETCH)
    chunk_before = jnp.concatenate([span_before[None], chunked[:-1, -1]])
    columns = [seg]
    columns += [seg == seg_ext[taps - 1 - back : taps - 1 - back + length] for back in range(1, taps)]
    columns += [
        (chunked == chunk_before[:, None]).reshape(-1),
        (chunked == chunked[:, -1:]).reshape(-1),
        seg == span_before,
    ]
    columns += [jnp.zeros_like(seg)] * (8 - len(columns))
    row_form = jnp.stack([column.astype(jnp.float32) for column in columns])
    row_seg = row_form
    aux = row_form.T
    bias = jnp.pad(step_bias[None], pad_heads)
    rate = jnp.pad(decay_rate[None], pad_heads)
    skip = jnp.repeat(skip_gain, head_dim)[None]
    matrix, before, aux, row_seg = lax.optimization_barrier((matrix, before, aux, row_seg))
    piece = lax.all_gather(normed, "tp", axis=0, tiled=True)
    piece, near = lax.optimization_barrier((piece, weights[:3]))
    projected = jnp.dot(piece, matrix, preferred_element_type=jnp.float32)
    y, c_map, w_span, packed = local_scan(
        heads_dev, state_dim, projected, before, aux, row_seg, filters.astype(jnp.float32),
        bias, rate, skip,
    )
    incoming = entering_state(packed, state_dim)
    gated, squares = gate_all(
        heads_dev, y, c_map, w_span, projected, conv_dim // inner_dev, incoming
    )
    gated, far = lax.optimization_barrier((gated, weights[3:]))
    weights = near + far
    own_squares = squares[:, 0]
    other_squares = swapped(own_squares, "tp", 0)
    group_mean = (own_squares + other_squares) / (2 * inner_dev)
    mixed = (gated * lax.rsqrt(group_mean + EPS)[:, None] * mixer_gain).astype(jnp.bfloat16)
    return project_out(hidden, mixed, weights)


def solution(mesh):
    in_specs = (
        P(("seq", "tp"), None),
        P(),
        P(None, None, "tp"),
        P(None, "tp"),
        P(None, "tp"),
        P("tp"),
        P("tp"),
        P(None, "tp"),
        P(None, "tp"),
        P("tp"),
        P("tp"),
        P("tp", None),
        P(),
    )
    out_specs = P(("seq", "tp"), None)
    return jax.shard_map(body, mesh=mesh, in_specs=in_specs, out_specs=out_specs, check_vma=False)
```

```python
import jax
import jax.numpy as jnp
from jax import lax
from jax.experimental import pallas as pl
from jax.experimental.pallas import tpu as pltpu
from jax.sharding import PartitionSpec as P

STRETCH = 128
LANES = 128


EPS = 1e-05
HIGH = lax.Precision.HIGHEST


def swapped(block, axis, stride):
    count = lax.axis_size(axis)
    route = []
    for low in range(count):
        high = low | 1 << stride
        if high != low and high < count:
            route += [(low, high), (high, low)]
    return lax.ppermute(block, axis, route)


def crossed(block, axis, mask):
    if mask == 0:
        return block
    return lax.ppermute(block, axis, [(i, i ^ mask) for i in range(lax.axis_size(axis))])


def tail_of_previous(block):
    spans, parts = lax.axis_size("seq"), lax.axis_size("tp")
    total = None
    for part in range(parts):
        route = [(i * parts - 1, i * parts + part) for i in range(1, spans)]
        got = lax.ppermute(block, ("seq", "tp"), route)
        total = got if total is None else total + got
    return total


def spread_along(weight, spans, chips):
    cols = weight.shape[1] // spans
    own = lax.dynamic_slice_in_dim(weight, lax.axis_index("seq") * cols, cols, axis=1)
    return [crossed(own, "tp", 2 * d) for d in range(chips)]


def silu(v):
    return v / (1.0 + jnp.exp(-v))


def widen(cols, heads, head_dim):
    rows = cols.shape[0]
    parts = [jnp.broadcast_to(cols[:, h : h + 1], (rows, head_dim)) for h in range(heads)]
    return jnp.concatenate(parts, axis=1)


def dot16(a, b, dims=((1,), (0,))):
    a, b = a.astype(jnp.bfloat16), b.astype(jnp.bfloat16)
    return lax.dot_general(a, b, (dims, ((), ())), preferred_element_type=jnp.float32)


def scan_kernel(
    heads, proj, before, aux, row_seg, taps, bias, rate, skip, y_out, c_out, w_out, s_out,
    edge, state, total,
):
    size, inner = y_out.shape
    states = c_out.shape[1]
    head_dim = inner // heads
    step_at = pl.program_id(0)

    @pl.when(step_at == 0)
    def _():
        edge[...] = before[...]
        state[...] = jnp.zeros_like(state)
        total[...] = jnp.zeros_like(total)

    conv = inner + 2 * states
    cur = proj[:, :conv]
    both = jnp.concatenate([edge[...], cur], axis=0)
    edge[...] = cur[size - 8 :]
    tap = taps[...]
    count = tap.shape[0]
    acc = tap[count - 1 : count] * cur
    for back in range(1, count):
        same = aux[:, back : back + 1]
        acc += tap[count - 1 - back : count - back] * both[8 - back : 8 - back + size] * same
    active = silu(acc)
    x = active[:, :inner]
    b_map = active[:, inner : inner + states]
    c_map = active[:, inner + states :]
    raw = proj[:, conv + inner :] + bias[...]
    step = jnp.maximum(raw, 0.0) + jnp.log1p(jnp.exp(-jnp.abs(raw)))
    log_decay = -step * rate[...]
    row_at = lax.broadcasted_iota(jnp.int32, (size, size), 0)
    col_at = lax.broadcasted_iota(jnp.int32, (size, size), 1)
    causal = row_at >= col_at
    cum = jnp.dot(
        causal.astype(jnp.float32), log_decay, precision=HIGH, preferred_element_type=jnp.float32
    )
    cum_rows = cum.T
    alive, in_last, alive_span = aux[:, 4:5], aux[:, 5:6], aux[:, 6:7]
    last = cum[size - 1 :]
    mask = causal & (aux[:, 0:1] == row_seg[0:1, :])
    xs = x * widen(step, heads, head_dim)
    xs16 = xs.astype(jnp.bfloat16)
    products = dot16(c_map, b_map, ((1,), (1,)))
    parts = []
    for h in range(heads):
        gap = cum[:, h : h + 1] - cum_rows[h : h + 1, :]
        mixing = products * jnp.exp(jnp.where(mask, gap, -1e30))
        parts.append(dot16(mixing, xs16[:, h * head_dim : (h + 1) * head_dim]))
    local = jnp.concatenate(parts, axis=1)
    entry = jnp.exp(cum) * alive
    carried = dot16(c_map, state[...]) * widen(entry, heads, head_dim)
    y_out[...] = local + carried + skip[...] * x
    c_out[...] = c_map.astype(jnp.bfloat16)
    w_span = jnp.exp(cum + total[...]) * alive_span
    w_out[...] = w_span
    end = jnp.exp(last - cum) * in_last
    fresh = dot16(b_map, xs * widen(end, heads, head_dim), ((0,), (0,)))
    state[...] = widen(entry[size - 1 :], heads, head_dim) * state[...] + fresh
    total[...] = total[...] + last

    @pl.when(step_at == pl.num_programs(0) - 1)
    def _():
        s_out[0:states] = state[...]
        s_out[states:] = jnp.broadcast_to(
            widen(w_span[size - 1 :], heads, head_dim), (8, inner)
        )


def local_scan(heads, states, proj, before, aux, row_seg, taps, bias, rate, skip):
    length = proj.shape[0]
    inner = skip.shape[1]
    whole = lambda a: pl.BlockSpec(a.shape, lambda i: (0,) * a.ndim)
    rows = lambda n: pl.BlockSpec((STRETCH, n), lambda i: (i, 0))
    return pl.pallas_call(
        lambda *refs: scan_kernel(heads, *refs),
        grid=(length // STRETCH,),
        in_specs=[
            rows(proj.shape[1]),
            whole(before),
            rows(aux.shape[1]),
            pl.BlockSpec((8, STRETCH), lambda i: (0, i)),
            whole(taps),
            whole(bias),
            whole(rate),
            whole(skip),
        ],
        out_specs=[
            rows(inner),
            rows(states),
            rows(LANES),
            pl.BlockSpec((states + 8, inner), lambda i: (0, 0)),
        ],
        out_shape=[
            jax.ShapeDtypeStruct((length, inner), jnp.float32),
            jax.ShapeDtypeStruct((length, states), jnp.bfloat16),
            jax.ShapeDtypeStruct((length, LANES), jnp.float32),
            jax.ShapeDtypeStruct((states + 8, inner), jnp.float32),
        ],
        scratch_shapes=[
            pltpu.VMEM((8, inner + 2 * states), jnp.float32),
            pltpu.VMEM((states, inner), jnp.float32),
            pltpu.VMEM((1, LANES), jnp.float32),
        ],
        compiler_params=pltpu.CompilerParams(vmem_limit_bytes=32 << 20),
        cost_estimate=pl.CostEstimate(
            flops=12_000_000_000, bytes_accessed=8_000_000, transcendentals=4_000_000
        ),
        name="local_scan",
    )(proj, before, aux, row_seg, taps, bias, rate, skip)


def gate_kernel(heads, y, c, w, gate, state, gated_out, sq_out):
    head_dim = y.shape[1] // heads
    carried = dot16(c[...], state[...]) * widen(w[...], heads, head_dim)
    gated = (y[...] + carried) * silu(gate[...])
    gated_out[...] = gated
    sq_out[...] = jnp.sum(gated * gated, axis=1, keepdims=True)


def gate_all(heads, y, c, w, proj, gate_block, state):
    length, inner = y.shape
    size = 256
    rows = lambda n: pl.BlockSpec((size, n), lambda i: (i, 0))
    return pl.pallas_call(
        lambda *refs: gate_kernel(heads, *refs),
        grid=(length // size,),
        in_specs=[
            rows(inner),
            rows(c.shape[1]),
            rows(LANES),
            pl.BlockSpec((size, inner), lambda i: (i, gate_block)),
            pl.BlockSpec(state.shape, lambda i: (0, 0)),
        ],
        out_specs=[rows(inner), rows(1)],
        out_shape=[
            jax.ShapeDtypeStruct((length, inner), jnp.float32),
            jax.ShapeDtypeStruct((length, 1), jnp.float32),
        ],
        compiler_params=pltpu.CompilerParams(vmem_limit_bytes=32 << 20),
        name="gate_all",
    )(y, c, w, proj, state)


def entering_state(packed, states):
    spans = lax.axis_size("seq")
    got = [
        lax.ppermute(packed, "seq", [(i, i + e) for i in range(spans - e)])
        for e in range(1, spans)
    ]
    total = jnp.zeros((states, packed.shape[1]), jnp.float32)
    for part in reversed(got):
        total = part[:states] + part[states : states + 1] * total
    return total


def project_out(hidden, mixed, weights):
    rows, spans, chips = hidden.shape[0], len(weights), len(weights[0])
    chip, core = lax.axis_index("tp") // 2, lax.axis_index("tp") % 2
    span = lax.axis_index("seq")
    cols = hidden.shape[1] // spans
    taken = []
    for d in range(chips):
        block = lax.dynamic_slice_in_dim(mixed, (chip ^ d) * 2 * rows, 2 * rows, axis=0)
        taken.append(crossed(block, "tp", 2 * d))
    out = jnp.zeros(hidden.shape, jnp.bfloat16)
    for e in range(spans):
        part = sum(
            jnp.dot(m, w, preferred_element_type=jnp.float32) for m, w in zip(taken, weights[e])
        )
        own = lax.dynamic_slice_in_dim(part, core * rows, rows, axis=0)
        other = lax.dynamic_slice_in_dim(part, (1 - core) * rows, rows, axis=0)
        other = crossed(other.astype(jnp.bfloat16), "tp", 1).astype(jnp.float32)
        start = (span ^ e) * cols
        base = lax.dynamic_slice_in_dim(hidden, start, cols, axis=1).astype(jnp.float32)
        done = (base + own + other).astype(jnp.bfloat16)
        out = lax.dynamic_update_slice_in_dim(out, done, start, axis=1)
    return out


def body(
    hidden,
    norm_gain,
    inner_weight,
    group_weight,
    step_weight,
    step_bias,
    decay_rate,
    filter_inner,
    filter_group,
    skip_gain,
    mixer_gain,
    output_weight,
    segment_ids,
):
    rows = hidden.shape[0]
    length = rows * lax.axis_size("tp")
    width = hidden.shape[1]
    inner_dev = inner_weight.shape[2]
    heads_dev = step_weight.shape[1]
    head_dim = inner_dev // heads_dev
    state_dim = group_weight.shape[1]
    taps = filter_inner.shape[0]
    first_row = lax.axis_index("seq") * length
    is_first = lax.axis_index("tp") % 2 == 0
    hidden_f = hidden.astype(jnp.float32)
    normed = (
        hidden_f
        * lax.rsqrt(jnp.mean(hidden_f * hidden_f, axis=-1, keepdims=True) + EPS)
        * norm_gain
    ).astype(jnp.bfloat16)
    other_weight, other_filter = swapped((group_weight, filter_group), "tp", 0)
    group_cols = (
        jnp.where(is_first, group_weight, other_weight),
        jnp.where(is_first, other_weight, group_weight),
    )
    filters = jnp.concatenate(
        [
            filter_inner,
            jnp.where(is_first, filter_group, other_filter),
            jnp.where(is_first, other_filter, filter_group),
        ],
        axis=1,
    )
    spans, chips = lax.axis_size("seq"), lax.axis_size("tp") // 2
    summed = width // 2
    tail = tail_of_previous(normed[rows - 8 :])
    pad_heads = ((0, 0), (0, LANES - heads_dev))
    matrix = jnp.concatenate(
        (inner_weight[:, 1, :],)
        + group_cols
        + (inner_weight[:, 0, :], jnp.pad(step_weight, pad_heads)),
        axis=1,
    )
    conv_dim = inner_dev + 2 * state_dim
    before = jnp.dot(tail, matrix[:, :conv_dim], preferred_element_type=jnp.float32)
    seg_pad = jnp.concatenate([jnp.full((taps - 1,), -1, jnp.int32), segment_ids])
    seg_ext = lax.dynamic_slice_in_dim(seg_pad, first_row, length + taps - 1)
    seg = seg_ext[taps - 1 :]
    span_before = seg_ext[taps - 2]
    chunked = seg.reshape(-1, STRETCH)
    chunk_before = jnp.concatenate([span_before[None], chunked[:-1, -1]])
    columns = [seg]
    columns += [seg == seg_ext[taps - 1 - back : taps - 1 - back + length] for back in range(1, taps)]
    columns += [
        (chunked == chunk_before[:, None]).reshape(-1),
        (chunked == chunked[:, -1:]).reshape(-1),
        seg == span_before,
    ]
    columns += [jnp.zeros_like(seg)] * (8 - len(columns))
    row_form = jnp.stack([column.astype(jnp.float32) for column in columns])
    row_seg = row_form
    aux = row_form.T
    bias = jnp.pad(step_bias[None], pad_heads)
    rate = jnp.pad(decay_rate[None], pad_heads)
    skip = jnp.repeat(skip_gain, head_dim)[None]
    matrix, before, aux, row_seg = lax.optimization_barrier((matrix, before, aux, row_seg))
    piece = lax.all_gather(normed, "tp", axis=0, tiled=True)
    piece, moved = lax.optimization_barrier((piece, output_weight[:, summed:]))
    along = spread_along(moved, spans, chips)
    projected = jnp.dot(piece, matrix, preferred_element_type=jnp.float32)
    y, c_map, w_span, packed = local_scan(
        heads_dev, state_dim, projected, before, aux, row_seg, filters.astype(jnp.float32),
        bias, rate, skip,
    )
    packed, along = lax.optimization_barrier((packed, along))
    incoming = entering_state(packed, state_dim)
    incoming, along = lax.optimization_barrier((incoming, along))
    weights = [[crossed(part, "seq", e) for part in along] for e in range(spans)]
    gated, squares = gate_all(
        heads_dev, y, c_map, w_span, projected, conv_dim // inner_dev, incoming
    )
    own_squares = squares[:, 0]
    other_squares = swapped(own_squares, "tp", 0)
    group_mean = (own_squares + other_squares) / (2 * inner_dev)
    mixed = (gated * lax.rsqrt(group_mean + EPS)[:, None] * mixer_gain).astype(jnp.bfloat16)
    partial_out = jnp.dot(
        mixed, output_weight[:, :summed], preferred_element_type=jnp.float32
    ).astype(jnp.bfloat16)
    mine = lax.psum_scatter(partial_out, "tp", scatter_dimension=0, tiled=True)
    right = project_out(hidden[:, summed:], mixed, weights)
    left = (hidden[:, :summed].astype(jnp.float32) + mine.astype(jnp.float32)).astype(jnp.bfloat16)
    return jnp.concatenate([left, right], axis=1)


def solution(mesh):
    in_specs = (
        P(("seq", "tp"), None),
        P(),
        P(None, None, "tp"),
        P(None, "tp"),
        P(None, "tp"),
        P("tp"),
        P("tp"),
        P(None, "tp"),
        P(None, "tp"),
        P("tp"),
        P("tp"),
        P("tp", None),
        P(),
    )
    out_specs = P(("seq", "tp"), None)
    return jax.shard_map(body, mesh=mesh, in_specs=in_specs, out_specs=out_specs, check_vma=False)
```

```python
import jax
import jax.numpy as jnp
from jax import lax
from jax.experimental import pallas as pl
from jax.experimental.pallas import tpu as pltpu
from jax.sharding import PartitionSpec as P

STRETCH = 128
LANES = 128


EPS = 1e-05
HIGH = lax.Precision.HIGHEST


def swapped(block, axis, stride):
    count = lax.axis_size(axis)
    route = []
    for low in range(count):
        high = low | 1 << stride
        if high != low and high < count:
            route += [(low, high), (high, low)]
    return lax.ppermute(block, axis, route)


def crossed(block, axis, mask):
    if mask == 0:
        return block
    return lax.ppermute(block, axis, [(i, i ^ mask) for i in range(lax.axis_size(axis))])


def tail_of_previous(block):
    spans, parts = lax.axis_size("seq"), lax.axis_size("tp")
    total = None
    for part in range(parts):
        route = [(i * parts - 1, i * parts + part) for i in range(1, spans)]
        got = lax.ppermute(block, ("seq", "tp"), route)
        total = got if total is None else total + got
    return total


def own_columns(weight, spans):
    cols = weight.shape[1] // spans
    return lax.dynamic_slice_in_dim(weight, lax.axis_index("seq") * cols, cols, axis=1)


def silu(v):
    return v / (1.0 + jnp.exp(-v))


def widen(cols, heads, head_dim):
    rows = cols.shape[0]
    parts = [jnp.broadcast_to(cols[:, h : h + 1], (rows, head_dim)) for h in range(heads)]
    return jnp.concatenate(parts, axis=1)


def dot16(a, b, dims=((1,), (0,))):
    a, b = a.astype(jnp.bfloat16), b.astype(jnp.bfloat16)
    return lax.dot_general(a, b, (dims, ((), ())), preferred_element_type=jnp.float32)


def scan_kernel(
    heads, proj, before, aux, row_seg, taps, bias, rate, skip, y_out, c_out, w_out, s_out,
    edge, state, total,
):
    size, inner = y_out.shape
    states = c_out.shape[1]
    head_dim = inner // heads
    step_at = pl.program_id(0)

    @pl.when(step_at == 0)
    def _():
        edge[...] = before[...]
        state[...] = jnp.zeros_like(state)
        total[...] = jnp.zeros_like(total)

    conv = inner + 2 * states
    cur = proj[:, :conv]
    both = jnp.concatenate([edge[...], cur], axis=0)
    edge[...] = cur[size - 8 :]
    tap = taps[...]
    count = tap.shape[0]
    acc = tap[count - 1 : count] * cur
    for back in range(1, count):
        same = aux[:, back : back + 1]
        acc += tap[count - 1 - back : count - back] * both[8 - back : 8 - back + size] * same
    active = silu(acc)
    x = active[:, :inner]
    b_map = active[:, inner : inner + states]
    c_map = active[:, inner + states :]
    raw = proj[:, conv + inner :] + bias[...]
    step = jnp.maximum(raw, 0.0) + jnp.log1p(jnp.exp(-jnp.abs(raw)))
    log_decay = -step * rate[...]
    row_at = lax.broadcasted_iota(jnp.int32, (size, size), 0)
    col_at = lax.broadcasted_iota(jnp.int32, (size, size), 1)
    causal = row_at >= col_at
    cum = jnp.dot(
        causal.astype(jnp.float32), log_decay, precision=HIGH, preferred_element_type=jnp.float32
    )
    cum_rows = cum.T
    alive, in_last, alive_span = aux[:, 4:5], aux[:, 5:6], aux[:, 6:7]
    last = cum[size - 1 :]
    mask = causal & (aux[:, 0:1] == row_seg[0:1, :])
    xs = x * widen(step, heads, head_dim)
    xs16 = xs.astype(jnp.bfloat16)
    products = dot16(c_map, b_map, ((1,), (1,)))
    parts = []
    for h in range(heads):
        gap = cum[:, h : h + 1] - cum_rows[h : h + 1, :]
        mixing = products * jnp.exp(jnp.where(mask, gap, -1e30))
        parts.append(dot16(mixing, xs16[:, h * head_dim : (h + 1) * head_dim]))
    local = jnp.concatenate(parts, axis=1)
    entry = jnp.exp(cum) * alive
    carried = dot16(c_map, state[...]) * widen(entry, heads, head_dim)
    y_out[...] = local + carried + skip[...] * x
    c_out[...] = c_map.astype(jnp.bfloat16)
    w_span = jnp.exp(cum + total[...]) * alive_span
    w_out[...] = w_span
    end = jnp.exp(last - cum) * in_last
    fresh = dot16(b_map, xs * widen(end, heads, head_dim), ((0,), (0,)))
    state[...] = widen(entry[size - 1 :], heads, head_dim) * state[...] + fresh
    total[...] = total[...] + last

    @pl.when(step_at == pl.num_programs(0) - 1)
    def _():
        s_out[0:states] = state[...]
        s_out[states:] = jnp.broadcast_to(
            widen(w_span[size - 1 :], heads, head_dim), (8, inner)
        )


def local_scan(heads, states, proj, before, aux, row_seg, taps, bias, rate, skip):
    length = proj.shape[0]
    inner = skip.shape[1]
    whole = lambda a: pl.BlockSpec(a.shape, lambda i: (0,) * a.ndim)
    rows = lambda n: pl.BlockSpec((STRETCH, n), lambda i: (i, 0))
    return pl.pallas_call(
        lambda *refs: scan_kernel(heads, *refs),
        grid=(length // STRETCH,),
        in_specs=[
            rows(proj.shape[1]),
            whole(before),
            rows(aux.shape[1]),
            pl.BlockSpec((8, STRETCH), lambda i: (0, i)),
            whole(taps),
            whole(bias),
            whole(rate),
            whole(skip),
        ],
        out_specs=[
            rows(inner),
            rows(states),
            rows(LANES),
            pl.BlockSpec((states + 8, inner), lambda i: (0, 0)),
        ],
        out_shape=[
            jax.ShapeDtypeStruct((length, inner), jnp.float32),
            jax.ShapeDtypeStruct((length, states), jnp.bfloat16),
            jax.ShapeDtypeStruct((length, LANES), jnp.float32),
            jax.ShapeDtypeStruct((states + 8, inner), jnp.float32),
        ],
        scratch_shapes=[
            pltpu.VMEM((8, inner + 2 * states), jnp.float32),
            pltpu.VMEM((states, inner), jnp.float32),
            pltpu.VMEM((1, LANES), jnp.float32),
        ],
        compiler_params=pltpu.CompilerParams(vmem_limit_bytes=32 << 20),
        cost_estimate=pl.CostEstimate(
            flops=12_000_000_000, bytes_accessed=8_000_000, transcendentals=4_000_000
        ),
        name="local_scan",
    )(proj, before, aux, row_seg, taps, bias, rate, skip)


def gate_kernel(heads, y, c, w, gate, state, gated_out, sq_out):
    head_dim = y.shape[1] // heads
    carried = dot16(c[...], state[...]) * widen(w[...], heads, head_dim)
    gated = (y[...] + carried) * silu(gate[...])
    gated_out[...] = gated
    sq_out[...] = jnp.sum(gated * gated, axis=1, keepdims=True)


def gate_all(heads, y, c, w, proj, gate_block, state):
    length, inner = y.shape
    size = 256
    rows = lambda n: pl.BlockSpec((size, n), lambda i: (i, 0))
    return pl.pallas_call(
        lambda *refs: gate_kernel(heads, *refs),
        grid=(length // size,),
        in_specs=[
            rows(inner),
            rows(c.shape[1]),
            rows(LANES),
            pl.BlockSpec((size, inner), lambda i: (i, gate_block)),
            pl.BlockSpec(state.shape, lambda i: (0, 0)),
        ],
        out_specs=[rows(inner), rows(1)],
        out_shape=[
            jax.ShapeDtypeStruct((length, inner), jnp.float32),
            jax.ShapeDtypeStruct((length, 1), jnp.float32),
        ],
        compiler_params=pltpu.CompilerParams(vmem_limit_bytes=32 << 20),
        name="gate_all",
    )(y, c, w, proj, state)


def entering_state(packed, states):
    spans = lax.axis_size("seq")
    got = [
        lax.ppermute(packed, "seq", [(i, i + e) for i in range(spans - e)])
        for e in range(1, spans)
    ]
    total = jnp.zeros((states, packed.shape[1]), jnp.float32)
    for part in reversed(got):
        total = part[:states] + part[states : states + 1] * total
    return total


def project_out(hidden, mixed, weights):
    rows, spans, chips = hidden.shape[0], len(weights), lax.axis_size("tp") // 2
    chip, core = lax.axis_index("tp") // 2, lax.axis_index("tp") % 2
    span = lax.axis_index("seq")
    cols = hidden.shape[1] // spans
    taken = []
    for d in range(chips):
        block = lax.dynamic_slice_in_dim(mixed, (chip ^ d) * 2 * rows, 2 * rows, axis=0)
        taken.append(crossed(block, "tp", 2 * d))
    taken = (taken[0], jnp.concatenate(taken[1:], axis=1))
    out = jnp.zeros(hidden.shape, jnp.bfloat16)
    for e in range(spans):
        part = sum(
            jnp.dot(m, w, preferred_element_type=jnp.float32) for m, w in zip(taken, weights[e])
        )
        own = lax.dynamic_slice_in_dim(part, core * rows, rows, axis=0)
        other = lax.dynamic_slice_in_dim(part, (1 - core) * rows, rows, axis=0)
        other = crossed(other.astype(jnp.bfloat16), "tp", 1).astype(jnp.float32)
        start = (span ^ e) * cols
        base = lax.dynamic_slice_in_dim(hidden, start, cols, axis=1).astype(jnp.float32)
        done = (base + own + other).astype(jnp.bfloat16)
        out = lax.dynamic_update_slice_in_dim(out, done, start, axis=1)
    return out


def body(
    hidden,
    norm_gain,
    inner_weight,
    group_weight,
    step_weight,
    step_bias,
    decay_rate,
    filter_inner,
    filter_group,
    skip_gain,
    mixer_gain,
    output_weight,
    segment_ids,
):
    rows = hidden.shape[0]
    length = rows * lax.axis_size("tp")
    width = hidden.shape[1]
    inner_dev = inner_weight.shape[2]
    heads_dev = step_weight.shape[1]
    head_dim = inner_dev // heads_dev
    state_dim = group_weight.shape[1]
    taps = filter_inner.shape[0]
    first_row = lax.axis_index("seq") * length
    is_first = lax.axis_index("tp") % 2 == 0
    hidden_f = hidden.astype(jnp.float32)
    normed = (
        hidden_f
        * lax.rsqrt(jnp.mean(hidden_f * hidden_f, axis=-1, keepdims=True) + EPS)
        * norm_gain
    ).astype(jnp.bfloat16)
    other_weight, other_filter = swapped((group_weight, filter_group), "tp", 0)
    group_cols = (
        jnp.where(is_first, group_weight, other_weight),
        jnp.where(is_first, other_weight, group_weight),
    )
    filters = jnp.concatenate(
        [
            filter_inner,
            jnp.where(is_first, filter_group, other_filter),
            jnp.where(is_first, other_filter, filter_group),
        ],
        axis=1,
    )
    spans, chips = lax.axis_size("seq"), lax.axis_size("tp") // 2
    summed = width - 3 * width // 8
    own = own_columns(output_weight[:, summed:], spans)
    first = [crossed(own, "seq", e) for e in range(spans)]
    tail = tail_of_previous(normed[rows - 8 :])
    pad_heads = ((0, 0), (0, LANES - heads_dev))
    matrix = jnp.concatenate(
        (inner_weight[:, 1, :],)
        + group_cols
        + (inner_weight[:, 0, :], jnp.pad(step_weight, pad_heads)),
        axis=1,
    )
    conv_dim = inner_dev + 2 * state_dim
    before = jnp.dot(tail, matrix[:, :conv_dim], preferred_element_type=jnp.float32)
    seg_pad = jnp.concatenate([jnp.full((taps - 1,), -1, jnp.int32), segment_ids])
    seg_ext = lax.dynamic_slice_in_dim(seg_pad, first_row, length + taps - 1)
    seg = seg_ext[taps - 1 :]
    span_before = seg_ext[taps - 2]
    chunked = seg.reshape(-1, STRETCH)
    chunk_before = jnp.concatenate([span_before[None], chunked[:-1, -1]])
    columns = [seg]
    columns += [seg == seg_ext[taps - 1 - back : taps - 1 - back + length] for back in range(1, taps)]
    columns += [
        (chunked == chunk_before[:, None]).reshape(-1),
        (chunked == chunked[:, -1:]).reshape(-1),
        seg == span_before,
    ]
    columns += [jnp.zeros_like(seg)] * (8 - len(columns))
    row_form = jnp.stack([column.astype(jnp.float32) for column in columns])
    row_seg = row_form
    aux = row_form.T
    bias = jnp.pad(step_bias[None], pad_heads)
    rate = jnp.pad(decay_rate[None], pad_heads)
    skip = jnp.repeat(skip_gain, head_dim)[None]
    matrix, before, aux, row_seg = lax.optimization_barrier((matrix, before, aux, row_seg))
    piece = lax.all_gather(normed, "tp", axis=0, tiled=True)
    piece, first, own = lax.optimization_barrier((piece, first, own))
    along = [crossed(own, "tp", 2 * d) for d in range(1, chips)]
    projected = jnp.dot(piece, matrix, preferred_element_type=jnp.float32)
    y, c_map, w_span, packed = local_scan(
        heads_dev, state_dim, projected, before, aux, row_seg, filters.astype(jnp.float32),
        bias, rate, skip,
    )
    packed, along = lax.optimization_barrier((packed, jnp.concatenate(along, axis=0)))
    incoming = entering_state(packed, state_dim)
    incoming, along = lax.optimization_barrier((incoming, along))
    weights = [(first[e], crossed(along, "seq", e)) for e in range(spans)]
    gated, squares = gate_all(
        heads_dev, y, c_map, w_span, projected, conv_dim // inner_dev, incoming
    )
    own_squares = squares[:, 0]
    other_squares = swapped(own_squares, "tp", 0)
    group_mean = (own_squares + other_squares) / (2 * inner_dev)
    mixed = (gated * lax.rsqrt(group_mean + EPS)[:, None] * mixer_gain).astype(jnp.bfloat16)
    partial_out = jnp.dot(
        mixed, output_weight[:, :summed], preferred_element_type=jnp.float32
    ).astype(jnp.bfloat16)
    mine = lax.psum_scatter(partial_out, "tp", scatter_dimension=0, tiled=True)
    right = project_out(hidden[:, summed:], mixed, weights)
    left = (hidden[:, :summed].astype(jnp.float32) + mine.astype(jnp.float32)).astype(jnp.bfloat16)
    return jnp.concatenate([left, right], axis=1)


def solution(mesh):
    in_specs = (
        P(("seq", "tp"), None),
        P(),
        P(None, None, "tp"),
        P(None, "tp"),
        P(None, "tp"),
        P("tp"),
        P("tp"),
        P(None, "tp"),
        P(None, "tp"),
        P("tp"),
        P("tp"),
        P("tp", None),
        P(),
    )
    out_specs = P(("seq", "tp"), None)
    return jax.shard_map(body, mesh=mesh, in_specs=in_specs, out_specs=out_specs, check_vma=False)
```

```python
import jax
import jax.numpy as jnp
from jax import lax
from jax.experimental import pallas as pl
from jax.experimental.pallas import tpu as pltpu
from jax.sharding import PartitionSpec as P

STRETCH = 128
LANES = 128


EPS = 1e-05
HIGH = lax.Precision.HIGHEST


def swapped(block, axis, stride):
    count = lax.axis_size(axis)
    route = []
    for low in range(count):
        high = low | 1 << stride
        if high != low and high < count:
            route += [(low, high), (high, low)]
    return lax.ppermute(block, axis, route)


def crossed(block, axis, mask):
    if mask == 0:
        return block
    return lax.ppermute(block, axis, [(i, i ^ mask) for i in range(lax.axis_size(axis))])


def tail_of_previous(block):
    spans, parts = lax.axis_size("seq"), lax.axis_size("tp")
    total = None
    for part in range(parts):
        route = [(i * parts - 1, i * parts + part) for i in range(1, spans)]
        got = lax.ppermute(block, ("seq", "tp"), route)
        total = got if total is None else total + got
    return total


def own_columns(weight, spans):
    cols = weight.shape[1] // spans
    return lax.dynamic_slice_in_dim(weight, lax.axis_index("seq") * cols, cols, axis=1)


def silu(v):
    return v / (1.0 + jnp.exp(-v))


def widen(cols, heads, head_dim):
    rows = cols.shape[0]
    parts = [jnp.broadcast_to(cols[:, h : h + 1], (rows, head_dim)) for h in range(heads)]
    return jnp.concatenate(parts, axis=1)


def dot16(a, b, dims=((1,), (0,))):
    a, b = a.astype(jnp.bfloat16), b.astype(jnp.bfloat16)
    return lax.dot_general(a, b, (dims, ((), ())), preferred_element_type=jnp.float32)


def scan_kernel(
    heads, proj, before, aux, row_seg, taps, bias, rate, skip, y_out, c_out, w_out, s_out,
    edge, state, total,
):
    size, inner = y_out.shape
    states = c_out.shape[1]
    head_dim = inner // heads
    step_at = pl.program_id(0)

    @pl.when(step_at == 0)
    def _():
        edge[...] = before[...]
        state[...] = jnp.zeros_like(state)
        total[...] = jnp.zeros_like(total)

    conv = inner + 2 * states
    cur = proj[:, :conv]
    both = jnp.concatenate([edge[...], cur], axis=0)
    edge[...] = cur[size - 8 :]
    tap = taps[...]
    count = tap.shape[0]
    acc = tap[count - 1 : count] * cur
    for back in range(1, count):
        same = aux[:, back : back + 1]
        acc += tap[count - 1 - back : count - back] * both[8 - back : 8 - back + size] * same
    active = silu(acc)
    x = active[:, :inner]
    b_map = active[:, inner : inner + states]
    c_map = active[:, inner + states :]
    raw = proj[:, conv + inner :] + bias[...]
    step = jnp.maximum(raw, 0.0) + jnp.log1p(jnp.exp(-jnp.abs(raw)))
    log_decay = -step * rate[...]
    row_at = lax.broadcasted_iota(jnp.int32, (size, size), 0)
    col_at = lax.broadcasted_iota(jnp.int32, (size, size), 1)
    causal = row_at >= col_at
    cum = jnp.dot(
        causal.astype(jnp.float32), log_decay, precision=HIGH, preferred_element_type=jnp.float32
    )
    cum_rows = cum.T
    alive, in_last, alive_span = aux[:, 4:5], aux[:, 5:6], aux[:, 6:7]
    last = cum[size - 1 :]
    mask = causal & (aux[:, 0:1] == row_seg[0:1, :])
    xs = x * widen(step, heads, head_dim)
    xs16 = xs.astype(jnp.bfloat16)
    products = dot16(c_map, b_map, ((1,), (1,)))
    parts = []
    for h in range(heads):
        gap = cum[:, h : h + 1] - cum_rows[h : h + 1, :]
        mixing = products * jnp.exp(jnp.where(mask, gap, -1e30))
        parts.append(dot16(mixing, xs16[:, h * head_dim : (h + 1) * head_dim]))
    local = jnp.concatenate(parts, axis=1)
    entry = jnp.exp(cum) * alive
    carried = dot16(c_map, state[...]) * widen(entry, heads, head_dim)
    y_out[...] = local + carried + skip[...] * x
    c_out[...] = c_map.astype(jnp.bfloat16)
    w_span = jnp.exp(cum + total[...]) * alive_span
    w_out[...] = w_span
    end = jnp.exp(last - cum) * in_last
    fresh = dot16(b_map, xs * widen(end, heads, head_dim), ((0,), (0,)))
    state[...] = widen(entry[size - 1 :], heads, head_dim) * state[...] + fresh
    total[...] = total[...] + last

    @pl.when(step_at == pl.num_programs(0) - 1)
    def _():
        s_out[0:states] = state[...]
        s_out[states:] = jnp.broadcast_to(
            widen(w_span[size - 1 :], heads, head_dim), (8, inner)
        )


def local_scan(heads, states, proj, before, aux, row_seg, taps, bias, rate, skip):
    length = proj.shape[0]
    inner = skip.shape[1]
    whole = lambda a: pl.BlockSpec(a.shape, lambda i: (0,) * a.ndim)
    rows = lambda n: pl.BlockSpec((STRETCH, n), lambda i: (i, 0))
    return pl.pallas_call(
        lambda *refs: scan_kernel(heads, *refs),
        grid=(length // STRETCH,),
        in_specs=[
            rows(proj.shape[1]),
            whole(before),
            rows(aux.shape[1]),
            pl.BlockSpec((8, STRETCH), lambda i: (0, i)),
            whole(taps),
            whole(bias),
            whole(rate),
            whole(skip),
        ],
        out_specs=[
            rows(inner),
            rows(states),
            rows(LANES),
            pl.BlockSpec((states + 8, inner), lambda i: (0, 0)),
        ],
        out_shape=[
            jax.ShapeDtypeStruct((length, inner), jnp.float32),
            jax.ShapeDtypeStruct((length, states), jnp.bfloat16),
            jax.ShapeDtypeStruct((length, LANES), jnp.float32),
            jax.ShapeDtypeStruct((states + 8, inner), jnp.float32),
        ],
        scratch_shapes=[
            pltpu.VMEM((8, inner + 2 * states), jnp.float32),
            pltpu.VMEM((states, inner), jnp.float32),
            pltpu.VMEM((1, LANES), jnp.float32),
        ],
        compiler_params=pltpu.CompilerParams(vmem_limit_bytes=32 << 20),
        cost_estimate=pl.CostEstimate(
            flops=12_000_000_000, bytes_accessed=8_000_000, transcendentals=4_000_000
        ),
        name="local_scan",
    )(proj, before, aux, row_seg, taps, bias, rate, skip)


def gate_kernel(heads, y, c, w, gate, state, gated_out, sq_out):
    head_dim = y.shape[1] // heads
    carried = dot16(c[...], state[...]) * widen(w[...], heads, head_dim)
    gated = (y[...] + carried) * silu(gate[...])
    gated_out[...] = gated
    sq_out[...] = jnp.sum(gated * gated, axis=1, keepdims=True)


def gate_all(heads, y, c, w, proj, gate_block, state):
    length, inner = y.shape
    size = 256
    rows = lambda n: pl.BlockSpec((size, n), lambda i: (i, 0))
    return pl.pallas_call(
        lambda *refs: gate_kernel(heads, *refs),
        grid=(length // size,),
        in_specs=[
            rows(inner),
            rows(c.shape[1]),
            rows(LANES),
            pl.BlockSpec((size, inner), lambda i: (i, gate_block)),
            pl.BlockSpec(state.shape, lambda i: (0, 0)),
        ],
        out_specs=[rows(inner), rows(1)],
        out_shape=[
            jax.ShapeDtypeStruct((length, inner), jnp.float32),
            jax.ShapeDtypeStruct((length, 1), jnp.float32),
        ],
        compiler_params=pltpu.CompilerParams(vmem_limit_bytes=32 << 20),
        name="gate_all",
    )(y, c, w, proj, state)


def entering_state(packed, states):
    spans = lax.axis_size("seq")
    got = [
        lax.ppermute(packed, "seq", [(i, i + e) for i in range(spans - e)])
        for e in range(1, spans)
    ]
    total = jnp.zeros((states, packed.shape[1]), jnp.float32)
    for part in reversed(got):
        total = part[:states] + part[states : states + 1] * total
    return total


def project_out(hidden, mixed, weights):
    rows, spans, chips = hidden.shape[0], len(weights), lax.axis_size("tp") // 2
    chip, core = lax.axis_index("tp") // 2, lax.axis_index("tp") % 2
    span = lax.axis_index("seq")
    cols = hidden.shape[1] // spans
    taken = []
    for d in range(chips):
        block = lax.dynamic_slice_in_dim(mixed, (chip ^ d) * 2 * rows, 2 * rows, axis=0)
        taken.append(crossed(block, "tp", 2 * d))
    taken = (taken[0], jnp.concatenate(taken[1:], axis=1))
    out = jnp.zeros(hidden.shape, jnp.bfloat16)
    for e in range(spans):
        part = sum(
            jnp.dot(m, w, preferred_element_type=jnp.float32) for m, w in zip(taken, weights[e])
        )
        own = lax.dynamic_slice_in_dim(part, core * rows, rows, axis=0)
        other = lax.dynamic_slice_in_dim(part, (1 - core) * rows, rows, axis=0)
        other = crossed(other.astype(jnp.bfloat16), "tp", 1).astype(jnp.float32)
        start = (span ^ e) * cols
        base = lax.dynamic_slice_in_dim(hidden, start, cols, axis=1).astype(jnp.float32)
        done = (base + own + other).astype(jnp.bfloat16)
        out = lax.dynamic_update_slice_in_dim(out, done, start, axis=1)
    return out


def body(
    hidden,
    norm_gain,
    inner_weight,
    group_weight,
    step_weight,
    step_bias,
    decay_rate,
    filter_inner,
    filter_group,
    skip_gain,
    mixer_gain,
    output_weight,
    segment_ids,
):
    rows = hidden.shape[0]
    length = rows * lax.axis_size("tp")
    width = hidden.shape[1]
    inner_dev = inner_weight.shape[2]
    heads_dev = step_weight.shape[1]
    head_dim = inner_dev // heads_dev
    state_dim = group_weight.shape[1]
    taps = filter_inner.shape[0]
    first_row = lax.axis_index("seq") * length
    is_first = lax.axis_index("tp") % 2 == 0
    hidden_f = hidden.astype(jnp.float32)
    normed = (
        hidden_f
        * lax.rsqrt(jnp.mean(hidden_f * hidden_f, axis=-1, keepdims=True) + EPS)
        * norm_gain
    ).astype(jnp.bfloat16)
    other_weight, other_filter = swapped((group_weight, filter_group), "tp", 0)
    group_cols = (
        jnp.where(is_first, group_weight, other_weight),
        jnp.where(is_first, other_weight, group_weight),
    )
    filters = jnp.concatenate(
        [
            filter_inner,
            jnp.where(is_first, filter_group, other_filter),
            jnp.where(is_first, other_filter, filter_group),
        ],
        axis=1,
    )
    spans, chips = lax.axis_size("seq"), lax.axis_size("tp") // 2
    summed = width // 2
    own = own_columns(output_weight[:, summed:], spans)
    first = [crossed(own, "seq", e) for e in range(spans)]
    tail = tail_of_previous(normed[rows - 8 :])
    pad_heads = ((0, 0), (0, LANES - heads_dev))
    matrix = jnp.concatenate(
        (inner_weight[:, 1, :],)
        + group_cols
        + (inner_weight[:, 0, :], jnp.pad(step_weight, pad_heads)),
        axis=1,
    )
    conv_dim = inner_dev + 2 * state_dim
    before = jnp.dot(tail, matrix[:, :conv_dim], preferred_element_type=jnp.float32)
    seg_pad = jnp.concatenate([jnp.full((taps - 1,), -1, jnp.int32), segment_ids])
    seg_ext = lax.dynamic_slice_in_dim(seg_pad, first_row, length + taps - 1)
    seg = seg_ext[taps - 1 :]
    span_before = seg_ext[taps - 2]
    chunked = seg.reshape(-1, STRETCH)
    chunk_before = jnp.concatenate([span_before[None], chunked[:-1, -1]])
    columns = [seg]
    columns += [seg == seg_ext[taps - 1 - back : taps - 1 - back + length] for back in range(1, taps)]
    columns += [
        (chunked == chunk_before[:, None]).reshape(-1),
        (chunked == chunked[:, -1:]).reshape(-1),
        seg == span_before,
    ]
    columns += [jnp.zeros_like(seg)] * (8 - len(columns))
    row_form = jnp.stack([column.astype(jnp.float32) for column in columns])
    row_seg = row_form
    aux = row_form.T
    bias = jnp.pad(step_bias[None], pad_heads)
    rate = jnp.pad(decay_rate[None], pad_heads)
    skip = jnp.repeat(skip_gain, head_dim)[None]
    matrix, before, aux, row_seg = lax.optimization_barrier((matrix, before, aux, row_seg))
    piece = lax.all_gather(normed, "tp", axis=0, tiled=True)
    piece, first, own = lax.optimization_barrier((piece, first, own))
    along = [crossed(own, "tp", 2 * d) for d in range(1, chips)]
    projected = jnp.dot(piece, matrix, preferred_element_type=jnp.float32)
    y, c_map, w_span, packed = local_scan(
        heads_dev, state_dim, projected, before, aux, row_seg, filters.astype(jnp.float32),
        bias, rate, skip,
    )
    packed, along = lax.optimization_barrier((packed, jnp.concatenate(along, axis=0)))
    incoming = entering_state(packed, state_dim)
    incoming, along = lax.optimization_barrier((incoming, along))
    weights = [(first[e], crossed(along, "seq", e)) for e in range(spans)]
    gated, squares = gate_all(
        heads_dev, y, c_map, w_span, projected, conv_dim // inner_dev, incoming
    )
    own_squares = squares[:, 0]
    other_squares = swapped(own_squares, "tp", 0)
    group_mean = (own_squares + other_squares) / (2 * inner_dev)
    mixed = (gated * lax.rsqrt(group_mean + EPS)[:, None] * mixer_gain).astype(jnp.bfloat16)
    partial_out = jnp.dot(
        mixed, output_weight[:, :summed], preferred_element_type=jnp.float32
    ).astype(jnp.bfloat16)
    mine = lax.psum_scatter(partial_out, "tp", scatter_dimension=0, tiled=True)
    right = project_out(hidden[:, summed:], mixed, weights)
    left = (hidden[:, :summed].astype(jnp.float32) + mine.astype(jnp.float32)).astype(jnp.bfloat16)
    return jnp.concatenate([left, right], axis=1)


def solution(mesh):
    in_specs = (
        P(("seq", "tp"), None),
        P(),
        P(None, None, "tp"),
        P(None, "tp"),
        P(None, "tp"),
        P("tp"),
        P("tp"),
        P(None, "tp"),
        P(None, "tp"),
        P("tp"),
        P("tp"),
        P("tp", None),
        P(),
    )
    out_specs = P(("seq", "tp"), None)
    return jax.shard_map(body, mesh=mesh, in_specs=in_specs, out_specs=out_specs, check_vma=False)
```
